32 devices in a mesh: grp: 8 (over y, x, core), blk: 4 (over z).
Axes of the slice: x: 2, y: 2, z: 4, core: 2. Of those that a mesh axis runs over, the one named last changes fastest.
Arguments:
- gradient: bfloat16 [2048, 4096], P(('grp', 'blk')), may hold values from -6 to 6
- stats_left: float32 [32, 512, 512], P(('grp', 'blk')), as said below
- stats_right: float32 [32, 512, 512], P(('grp', 'blk')), as said below
- root_left: bfloat16 [32, 512, 512], P(('grp', 'blk')), may hold values from -0.25 to 0.25
- root_right: bfloat16 [32, 512, 512], P(('grp', 'blk')), may hold values from -0.25 to 0.25
- slot_block: int32 [8, 4], replicated, may hold values from 0 to 3, each once within a row
- refresh_slots: int32 [4], replicated, may hold values from 0 to 31, as said below
- newton_steps: int32 [4], replicated, may hold values from 1 to 3, as said below
Outputs:
- new_left: float32 [32, 512, 512], P(('grp', 'blk'))
- new_right: float32 [32, 512, 512], P(('grp', 'blk'))
- new_root_left: bfloat16 [32, 512, 512], P(('grp', 'blk'))
- new_root_right: bfloat16 [32, 512, 512], P(('grp', 'blk'))
- update: bfloat16 [2048, 4096], P(('grp', 'blk'))
The draws below stay inside these ranges and needn't reach their ends.
Inputs may be any that keep to these rules, and one draw needn't show every extreme that they name: `stats_left`: each matrix is symmetric positive definite. `stats_right`: each matrix is symmetric positive definite. `slot_block`: row c lists each block row once. `refresh_slots`: distinct slot numbers. `newton_steps`: not all elements are equal.
All inputs are finite; a program needn't handle non-finite values.
Results may differ from the reference program's by a relative error of at most 0.0051.
Values may be sent and summed in bfloat16 or wider, within the bound.
A program may use at most 64 MiB of HBM per device.

```python
import jax
import jax.numpy as jnp
from jax import lax

B = 512
NEWTON = 3
ROWS = 2048
COLS = 4096
NBLOCKS = 32
NREF = 4
N_GRP = 8
N_BLK = 4


def definite_blocks(key):
    full_shape = (NBLOCKS, B, B)
    spread_key, noise_key = jax.random.split(key, 2)
    log_scale = jax.random.uniform(spread_key, (NBLOCKS, B), minval=jnp.log(0.1), maxval=jnp.log(2.0))
    diagonal = jnp.exp(log_scale)
    noise_field = jax.random.uniform(noise_key, full_shape, minval=-1.0, maxval=1.0)
    upper_part = jnp.triu(noise_field, 1)
    coupling_limit = 0.8 / B
    unit_matrix = coupling_limit * (upper_part + jnp.swapaxes(upper_part, 1, 2)) + jnp.eye(B, dtype=jnp.float32)
    square_root = jnp.sqrt(diagonal)
    return (square_root[:, :, None] * unit_matrix * square_root[:, None, :]).astype(jnp.float32)


def draw_stats_left(key, part):
    return definite_blocks(jax.random.fold_in(key, 17))


def draw_stats_right(key, part):
    return definite_blocks(jax.random.fold_in(key, 29))


def draw_refresh_slots(key, part):
    base_key = jax.random.fold_in(key, 43)
    pick_key, order_key = jax.random.split(base_key, 2)
    middle = 1 + jax.random.permutation(pick_key, NBLOCKS - 2)[:NREF - 2]
    ends = jnp.array([0, NBLOCKS - 1], dtype=jnp.int32)
    chosen = jnp.concatenate([ends, middle.astype(jnp.int32)])
    return jax.random.permutation(order_key, chosen).astype(jnp.int32)


def draw_newton_steps(key, part):
    base_key = jax.random.fold_in(key, 59)
    values_key, order_key = jax.random.split(base_key, 2)
    values = jax.random.randint(values_key, (NREF,), 1, NEWTON + 1, dtype=jnp.int32)
    values = values.at[0].set(1).at[1].set(NEWTON)
    return jax.random.permutation(order_key, values).astype(jnp.int32)


def level_of(rng, shape, cuts, smallest, top_value):
    factor_of = 1.0
    for position, shards_of in cuts:
        steps = jax.random.uniform(jax.random.fold_in(jax.random.fold_in(rng, 6), position), (shards_of,), jnp.float32, smallest / len(cuts), top_value / len(cuts))
        factor_of = factor_of * jnp.repeat(jnp.exp(steps), shape[position] // shards_of).reshape((-1,) + (1,) * (len(shape) - 1 - position))
    return factor_of


def gaussian(key, extent, deviation, reach, shards=(), held_as=jnp.bfloat16):
    values = deviation * jax.random.normal(key, extent, jnp.float32)
    if shards:
        values = values * level_of(key, extent, shards, -0.22, 0.18)
    return jnp.clip(values, -reach, reach).astype(held_as)


def setup_inputs(seed: int = 0) -> dict:
    key_of = jax.random.split(jax.random.key(seed), 9)
    return {
        "gradient": gaussian(key_of[0], (ROWS, COLS), 1.0, 6.0, ((0, 32),)),
        "stats_left": draw_stats_left(jax.random.fold_in(key_of[8], 71), 0),
        "stats_right": draw_stats_right(jax.random.fold_in(key_of[8], 71), 0),
        "root_left": gaussian(key_of[3], (NBLOCKS, B, B), B ** -0.5, 0.25, ((0, 32),)),
        "root_right": gaussian(key_of[4], (NBLOCKS, B, B), B ** -0.5, 0.25, ((0, 32),)),
        "slot_block": jax.vmap(lambda own: jax.random.permutation(own, N_BLK))(jax.random.split(key_of[5], N_GRP)).reshape((N_GRP, N_BLK)).astype(jnp.int32),
        "refresh_slots": draw_refresh_slots(jax.random.fold_in(key_of[8], 71), 0),
        "newton_steps": draw_newton_steps(jax.random.fold_in(key_of[8], 71), 0),
    }


damping = 0.0001
decay_rate = 0.9
root_order = 4.0

def product(left, right):
    return jnp.dot(left, right, precision=lax.Precision.HIGHEST, preferred_element_type=jnp.float32)

def inverse_root(statistic, step_count):
    identity_matrix = jnp.eye(B, dtype=jnp.float32)
    shifted = statistic + damping * identity_matrix
    frobenius = jnp.sqrt(jnp.sum(shifted * shifted))
    scaling = (1.0 + root_order) / (2.0 * frobenius)
    iterate = scaling ** (1.0 / root_order) * identity_matrix
    moving = scaling * shifted

    def newton(unused, state_pair):
        iterate, moving = state_pair
        factor = ((root_order + 1.0) * identity_matrix - moving) / root_order
        iterate = product(iterate, factor)
        factor_sq = product(factor, factor)
        moving = product(product(factor_sq, factor_sq), moving)
        return (iterate, moving)
    return lax.fori_loop(0, step_count, newton, (iterate, moving))[0]

def one_slot(items):
    grad_block, left_old, right_old, left_stored, right_stored, step_count = items
    gram_weight = (1.0 - decay_rate) / B
    left_new = decay_rate * left_old + gram_weight * jnp.dot(grad_block, grad_block.T, preferred_element_type=jnp.float32)
    right_new = decay_rate * right_old + gram_weight * jnp.dot(grad_block.T, grad_block, preferred_element_type=jnp.float32)
    refreshed = step_count > 0
    left_root = jnp.where(refreshed, inverse_root(left_new, step_count).astype(jnp.bfloat16), left_stored)
    right_root = jnp.where(refreshed, inverse_root(right_new, step_count).astype(jnp.bfloat16), right_stored)
    half_product = jnp.dot(grad_block, right_root, preferred_element_type=jnp.float32).astype(jnp.bfloat16)
    precon = jnp.dot(left_root, half_product, preferred_element_type=jnp.float32)
    grad_wide = grad_block.astype(jnp.float32)
    graft_ratio = jnp.sqrt(jnp.mean(grad_wide * grad_wide)) / jnp.sqrt(jnp.mean(precon * precon) + 1e-06)
    update_block = (precon * graft_ratio).astype(jnp.bfloat16)
    return (left_new, right_new, left_root, right_root, update_block)

def reference(gradient, stats_left, stats_right, root_left, root_right, slot_block, refresh_slots, newton_steps):
    blocks = gradient.reshape(N_BLK, B, N_GRP, B).transpose(2, 0, 1, 3)
    column_ids = jnp.arange(N_GRP, dtype=jnp.int32)[:, None]
    slot_grads = blocks[column_ids, slot_block.astype(jnp.int32)].reshape(NBLOCKS, B, B)
    slot_steps = jnp.zeros((NBLOCKS,), jnp.int32).at[refresh_slots].set(newton_steps)
    left_new, right_new, left_root, right_root, updates = lax.map(one_slot, (slot_grads, stats_left, stats_right, root_left, root_right, slot_steps))
    placed = jnp.zeros((N_GRP, N_BLK, B, B), jnp.bfloat16)
    placed = placed.at[column_ids, slot_block.astype(jnp.int32)].set(updates.reshape(N_GRP, N_BLK, B, B))
    update = placed.transpose(1, 2, 0, 3).reshape(N_BLK * B, N_GRP * B)
    return (left_new, right_new, left_root, right_root, update)
```

```python
import functools

import jax
import jax.numpy as jnp
from jax import lax
from jax.experimental import pallas as pl
from jax.experimental.pallas import tpu as pltpu
from jax.sharding import PartitionSpec as P

damping = 0.0001
decay_rate = 0.9
root_order = 4.0
CHUNKS = 2
MESH = pl.DeviceIdType.MESH
F32 = jnp.float32
BF16 = jnp.bfloat16


def enter(groups, owners, grp, blk):
    barrier = pltpu.get_barrier_semaphore()
    for step in range(1, groups):
        peer = lax.rem(grp + step, groups)
        pl.semaphore_signal(barrier, inc=1, device_id=(peer, blk), device_id_type=MESH)
    for step in range(1, owners):
        peer = lax.rem(blk + step, owners)
        pl.semaphore_signal(barrier, inc=1, device_id=(grp, peer), device_id_type=MESH)
    pl.semaphore_wait(barrier, groups + owners - 2)


def remote(src, dst, send, recv, device):
    return pltpu.make_async_remote_copy(
        src_ref=src,
        dst_ref=dst,
        send_sem=send,
        recv_sem=recv,
        device_id=device,
        device_id_type=MESH,
    )


def inbound(groups, owners, order, x, g, landed, staged, local1, local2, s1, r1, s2, r2):
    grp, blk = lax.axis_index("grp"), lax.axis_index("blk")
    share = groups // owners
    block = landed[0].shape[-1] * CHUNKS
    width = landed[0].shape[-1]

    def columns(owner, chunk):
        return pl.ds(pl.multiple_of(owner * block + chunk * width, width), width)

    mine = []
    for chunk in range(CHUNKS):
        copy = pltpu.make_async_copy(
            x.at[:, columns(grp, chunk)], landed[chunk].at[grp], local1.at[chunk]
        )
        copy.start()
        mine.append(copy)
    enter(groups, owners, grp, blk)
    first = []
    for chunk in range(CHUNKS):
        row = []
        for step in range(1, groups):
            peer = lax.rem(grp + step, groups)
            copy = remote(
                x.at[:, columns(peer, chunk)],
                landed[chunk].at[grp],
                s1.at[chunk, step],
                r1.at[chunk, step],
                (peer, blk),
            )
            copy.start()
            row.append(copy)
        first.append(row)
    second = []
    for chunk in range(CHUNKS):
        mine[chunk].wait()
        for copy in first[chunk]:
            copy.wait_recv()
        cut = pl.ds(chunk * width, width)
        for step in range(1, owners + 1):
            peer = lax.rem(blk + step, owners)
            source = order[grp, peer] * share
            staged[chunk, peer] = landed[chunk][pl.ds(source, share)]
            if step < owners:
                copy = remote(
                    staged.at[chunk, peer],
                    g.at[:, blk, :, cut],
                    s2.at[chunk, step],
                    r2.at[chunk, step],
                    (grp, peer),
                )
            else:
                copy = pltpu.make_async_copy(
                    staged.at[chunk, blk], g.at[:, blk, :, cut], local2.at[chunk]
                )
            copy.start()
            second.append((copy, step < owners))
    for copy, far in second:
        copy.wait()
    for row in first:
        for copy in row:
            copy.wait_send()


def outbound(groups, owners, order, u, y, landed, staged, local1, local2, s1, r1, s2, r2):
    grp, blk = lax.axis_index("grp"), lax.axis_index("blk")
    share = groups // owners
    width = landed[0].shape[-1]
    block = width * CHUNKS

    def columns(owner, chunk):
        return pl.ds(pl.multiple_of(owner * block + chunk * width, width), width)

    enter(groups, owners, grp, blk)
    first = []
    for chunk in range(CHUNKS):
        row = []
        cut = pl.ds(chunk * width, width)
        for step in range(1, owners):
            peer = lax.rem(blk + step, owners)
            copy = remote(
                u.at[:, peer, :, cut],
                landed[chunk].at[blk],
                s1.at[chunk, step],
                r1.at[chunk, step],
                (grp, peer),
            )
            copy.start()
            row.append(copy)
        copy = pltpu.make_async_copy(
            u.at[:, blk, :, cut], landed[chunk].at[blk], local1.at[chunk]
        )
        copy.start()
        first.append((row, copy))
    places = []
    for position in range(owners):
        place = jnp.int32(0)
        for slot in range(owners):
            place = jnp.where(order[grp, slot] == position, slot, place)
        places.append(place)
    second = []
    for chunk in range(CHUNKS):
        row, copy = first[chunk]
        copy.wait()
        for copy in row:
            copy.wait_recv()
        for position in range(owners):
            for part in range(share):
                staged[chunk, position * share + part] = landed[chunk][places[position], part]
        for step in range(1, groups + 1):
            peer = lax.rem(grp + step, groups)
            if step < groups:
                copy = remote(
                    staged.at[chunk, peer],
                    y.at[:, columns(grp, chunk)],
                    s2.at[chunk, step],
                    r2.at[chunk, step],
                    (peer, blk),
                )
            else:
                copy = pltpu.make_async_copy(
                    staged.at[chunk, grp], y.at[:, columns(grp, chunk)], local2.at[chunk]
                )
            copy.start()
            second.append(copy)
    for copy in second:
        copy.wait()
    for row, copy in first:
        for copy in row:
            copy.wait_send()


def product(left, right):
    return jnp.dot(left.astype(BF16), right.astype(BF16), preferred_element_type=F32)


def local(
    owners,
    picks,
    slots,
    steps,
    g,
    left_old,
    right_old,
    left_stored,
    right_stored,
    left_out,
    right_out,
    left_root,
    right_root,
    u,
    stats,
    roots,
    moving,
    iterate,
    in_sem,
    root_sem,
    out_sem,
    done_sem,
):
    size = g.shape[0]
    loads, root_loads = [], []
    for side, ref in enumerate((left_old, right_old)):
        loads.append(pltpu.make_async_copy(ref, stats.at[side], in_sem.at[side]))
        loads[-1].start()
    for side, ref in enumerate((left_stored, right_stored)):
        root_loads.append(pltpu.make_async_copy(ref, roots.at[side], root_sem.at[side]))
        root_loads[-1].start()
    mine = lax.axis_index("grp") * owners + lax.axis_index("blk")
    count = jnp.int32(0)
    for pick in range(picks):
        count = count + jnp.where(slots[pick] == mine, steps[pick], 0)
    weight = (1.0 - decay_rate) / size
    stores = []
    for side, (dims, ref) in enumerate(((1, left_out), (0, right_out))):
        gram = lax.dot_general(
            g[...], g[...], (((dims,), (dims,)), ((), ())), preferred_element_type=F32
        )
        loads[side].wait()
        stats[side] = decay_rate * stats[side] + weight * gram
        stores.append(pltpu.make_async_copy(stats.at[side], ref, out_sem.at[side]))
        stores[-1].start()
    for copy in root_loads:
        copy.wait()

    lead = (root_order + 1.0) / root_order
    square = lead * lead

    def unit(scale):
        rows = lax.broadcasted_iota(jnp.int32, (size, size), 0)
        cols = lax.broadcasted_iota(jnp.int32, (size, size), 1)
        return jnp.where(rows == cols, jnp.float32(scale), jnp.float32(0.0))

    def advance(m):
        part = product(m, m) / root_order**2 - (2.0 * lead / root_order) * m
        fourth = 2.0 * square * part + product(part, part)
        return square * square * m + product(fourth, m)

    @pl.when(count > 0)
    def refresh():
        scales = []
        for side in range(2):
            shifted = stats[side] + unit(damping)
            frobenius = jnp.sqrt(jnp.full((1, 1), jnp.sum(shifted * shifted), F32))
            scaling = (1.0 + root_order) / (2.0 * frobenius)
            scales.append(jnp.sqrt(jnp.sqrt(scaling)))
            moving[side] = scaling * shifted
            iterate[side] = unit(lead) - moving[side] / root_order

        @pl.when(count > 1)
        def again():
            for side in range(2):
                m = moving[side]
                after = advance(m)
                both = lead * after - product(m, after) / root_order
                moving[side] = after
                iterate[side] = lead * iterate[side] - both / root_order

        @pl.when(count > 2)
        def last():
            for side in range(2):
                y = iterate[side]
                iterate[side] = lead * y - product(y, advance(moving[side])) / root_order

        for side in range(2):
            roots[side] = (scales[side] * iterate[side]).astype(BF16)

    for side, ref in enumerate((left_root, right_root)):
        stores.append(pltpu.make_async_copy(roots.at[side], ref, done_sem.at[side]))
        stores[-1].start()
    half = jnp.dot(g[...], roots[1], preferred_element_type=F32).astype(BF16)
    precon = jnp.dot(roots[0], half, preferred_element_type=F32)
    wide = g[...].astype(F32)
    area = float(size * size)
    top = jnp.full((1, 1), jnp.sum(wide * wide), F32) / area
    bottom = jnp.full((1, 1), jnp.sum(precon * precon), F32) / area
    ratio = jnp.sqrt(top) / jnp.sqrt(bottom + 1e-06)
    u[...] = (precon * ratio).astype(BF16)
    for copy in stores:
        copy.wait()


ANY = pl.BlockSpec(memory_space=pl.ANY)
SMEM = pl.BlockSpec(memory_space=pltpu.SMEM)
VMEM = pl.BlockSpec(memory_space=pltpu.VMEM)
DMA = pltpu.SemaphoreType.DMA


def per_device(
    gradient,
    stats_left,
    stats_right,
    root_left,
    root_right,
    slot_block,
    refresh_slots,
    newton_steps,
):
    groups = lax.axis_size("grp")
    owners = lax.axis_size("blk")
    rows = gradient.shape[0]
    size = stats_left.shape[1]
    share = groups // owners
    width = size // CHUNKS
    g = pl.pallas_call(
        functools.partial(inbound, groups, owners),
        name="inbound",
        out_shape=jax.ShapeDtypeStruct((share, owners, rows, size), BF16),
        in_specs=[SMEM, ANY],
        out_specs=ANY,
        scratch_shapes=[
            [pltpu.VMEM((groups, rows, width), BF16)] * CHUNKS,
            pltpu.VMEM((CHUNKS, owners, share, rows, width), BF16),
            DMA((CHUNKS,)),
            DMA((CHUNKS,)),
            DMA((CHUNKS, groups)),
            DMA((CHUNKS, groups)),
            DMA((CHUNKS, owners)),
            DMA((CHUNKS, owners)),
        ],
        compiler_params=pltpu.CompilerParams(collective_id=0, has_side_effects=True),
    )(slot_block, gradient)
    square = jax.ShapeDtypeStruct((size, size), F32)
    narrow = jax.ShapeDtypeStruct((size, size), BF16)
    left_new, right_new, left_root, right_root, u = pl.pallas_call(
        functools.partial(local, owners, refresh_slots.shape[0]),
        name="local",
        out_shape=(square, square, narrow, narrow, narrow),
        in_specs=[SMEM, SMEM, VMEM, ANY, ANY, ANY, ANY],
        out_specs=(ANY, ANY, ANY, ANY, VMEM),
        scratch_shapes=[
            pltpu.VMEM((2, size, size), F32),
            pltpu.VMEM((2, size, size), BF16),
            pltpu.VMEM((2, size, size), F32),
            pltpu.VMEM((2, size, size), F32),
            DMA((2,)),
            DMA((2,)),
            DMA((2,)),
            DMA((2,)),
        ],
        compiler_params=pltpu.CompilerParams(vmem_limit_bytes=48 * 2**20),
    )(
        refresh_slots,
        newton_steps,
        g.reshape(size, size),
        stats_left[0],
        stats_right[0],
        root_left[0],
        root_right[0],
    )
    y = pl.pallas_call(
        functools.partial(outbound, groups, owners),
        name="outbound",
        out_shape=jax.ShapeDtypeStruct(gradient.shape, BF16),
        in_specs=[SMEM, ANY],
        out_specs=ANY,
        scratch_shapes=[
            [pltpu.VMEM((owners, share, rows, width), BF16)] * CHUNKS,
            pltpu.VMEM((CHUNKS, groups, rows, width), BF16),
            DMA((CHUNKS,)),
            DMA((CHUNKS,)),
            DMA((CHUNKS, owners)),
            DMA((CHUNKS, owners)),
            DMA((CHUNKS, groups)),
            DMA((CHUNKS, groups)),
        ],
        compiler_params=pltpu.CompilerParams(collective_id=1, has_side_effects=True),
    )(slot_block, u.reshape(share, owners, rows, size))
    return (left_new[None], right_new[None], left_root[None], right_root[None], y)


def solution(mesh):
    placed = (
        P(("grp", "blk"), None),
        P(("grp", "blk"), None, None),
        P(("grp", "blk"), None, None),
        P(("grp", "blk"), None, None),
        P(("grp", "blk"), None, None),
        P(),
        P(),
        P(),
    )
    return jax.shard_map(
        per_device,
        mesh=mesh,
        in_specs=placed,
        out_specs=(
            P(("grp", "blk"), None, None),
            P(("grp", "blk"), None, None),
            P(("grp", "blk"), None, None),
            P(("grp", "blk"), None, None),
            P(("grp", "blk"), None),
        ),
        check_vma=False,
    )
```

```python
import functools

import jax
import jax.numpy as jnp
from jax import lax
from jax.experimental import pallas as pl
from jax.experimental.pallas import tpu as pltpu
from jax.sharding import PartitionSpec as P

damping = 0.0001
decay_rate = 0.9
root_order = 4.0
CHUNKS = 4
GRANT = 28 * 2**20
SMALL = 12 * 2**20
WIDE = 12 * 2**20
MESH = pl.DeviceIdType.MESH
F32 = jnp.float32
BF16 = jnp.bfloat16


def enter(groups, owners, grp, blk):
    barrier = pltpu.get_barrier_semaphore()
    for step in range(1, groups):
        peer = lax.rem(grp + step, groups)
        pl.semaphore_signal(barrier, inc=1, device_id=(peer, blk), device_id_type=MESH)
    for step in range(1, owners):
        peer = lax.rem(blk + step, owners)
        pl.semaphore_signal(barrier, inc=1, device_id=(grp, peer), device_id_type=MESH)
    pl.semaphore_wait(barrier, groups + owners - 2)


def remote(src, dst, send, recv, device):
    return pltpu.make_async_remote_copy(
        src_ref=src,
        dst_ref=dst,
        send_sem=send,
        recv_sem=recv,
        device_id=device,
        device_id_type=MESH,
    )


def inbound(groups, owners, picks, *refs):
    table, slots_in, steps_in, x = refs[:4]
    held_in, held = refs[4:8], refs[10:14]
    g, info = refs[8:10]
    order, slots, steps, landed, staged, local1, local2, s1, r1, s2, r2, small, large = refs[14:]
    grp, blk = lax.axis_index("grp"), lax.axis_index("blk")
    tables = []
    for place, (source, target) in enumerate(((table, order), (slots_in, slots), (steps_in, steps))):
        tables.append(pltpu.make_async_copy(source, target, small.at[place]))
        tables[-1].start()
    share = groups // owners
    block = landed[0].shape[-1] * CHUNKS
    width = landed[0].shape[-1]

    def columns(owner, chunk):
        return pl.ds(pl.multiple_of(owner * block + chunk * width, width), width)

    mine = []
    for chunk in range(CHUNKS):
        copy = pltpu.make_async_copy(
            x.at[:, columns(grp, chunk)], landed[chunk].at[grp], local1.at[chunk]
        )
        copy.start()
        mine.append(copy)
    enter(groups, owners, grp, blk)
    first = []
    for chunk in range(CHUNKS):
        row = []
        for step in range(1, groups):
            peer = lax.rem(grp + step, groups)
            copy = remote(
                x.at[:, columns(peer, chunk)],
                landed[chunk].at[grp],
                s1.at[chunk, step],
                r1.at[chunk, step],
                (peer, blk),
            )
            copy.start()
            row.append(copy)
        first.append(row)
    loads = []
    for place in range(4):
        loads.append(pltpu.make_async_copy(held_in[place], held[place], large.at[place]))
        loads[-1].start()
    for copy in tables:
        copy.wait()
    own = grp * owners + blk
    count = jnp.int32(0)
    for pick in range(picks):
        count = count + jnp.where(slots[pick] == own, steps[pick], 0)
    info[...] = jnp.full(info.shape, count, jnp.int32)
    second = []
    for chunk in range(CHUNKS):
        mine[chunk].wait()
        for copy in first[chunk]:
            copy.wait_recv()
        cut = pl.ds(chunk * width, width)
        for step in range(1, owners + 1):
            peer = lax.rem(blk + step, owners)
            source = order[peer, grp] * share
            staged[chunk, peer] = landed[chunk][pl.ds(source, share)]
            if step < owners:
                copy = remote(
                    staged.at[chunk, peer],
                    g.at[:, blk, :, cut],
                    s2.at[chunk, step],
                    r2.at[chunk, step],
                    (grp, peer),
                )
            else:
                copy = pltpu.make_async_copy(
                    staged.at[chunk, blk], g.at[:, blk, :, cut], local2.at[chunk]
                )
            copy.start()
            second.append(copy)
    for copy in second:
        copy.wait()
    for copy in loads:
        copy.wait()
    for row in first:
        for copy in row:
            copy.wait_send()


def outbound(
    groups, owners, table, u, y, order, landed, staged, local1, local2, s1, r1, s2, r2, small
):
    grp, blk = lax.axis_index("grp"), lax.axis_index("blk")
    fetch = pltpu.make_async_copy(table, order, small)
    fetch.start()
    share = groups // owners
    width = landed[0].shape[-1]
    block = width * CHUNKS

    def columns(owner, chunk):
        return pl.ds(pl.multiple_of(owner * block + chunk * width, width), width)

    enter(groups, owners, grp, blk)
    first = []
    for chunk in range(CHUNKS):
        row = []
        cut = pl.ds(chunk * width, width)
        for step in range(1, owners):
            peer = lax.rem(blk + step, owners)
            copy = remote(
                u.at[:, peer, :, cut],
                landed[chunk].at[blk],
                s1.at[chunk, step],
                r1.at[chunk, step],
                (grp, peer),
            )
            copy.start()
            row.append(copy)
        copy = pltpu.make_async_copy(
            u.at[:, blk, :, cut], landed[chunk].at[blk], local1.at[chunk]
        )
        copy.start()
        first.append((row, copy))
    fetch.wait()
    places = []
    for position in range(owners):
        place = jnp.int32(0)
        for slot in range(owners):
            place = jnp.where(order[slot, grp] == position, slot, place)
        places.append(place)
    second = []
    for chunk in range(CHUNKS):
        row, copy = first[chunk]
        copy.wait()
        for copy in row:
            copy.wait_recv()
        for position in range(owners):
            for part in range(share):
                staged[chunk, position * share + part] = landed[chunk][places[position], part]
        for step in range(1, groups + 1):
            peer = lax.rem(grp + step, groups)
            if step < groups:
                copy = remote(
                    staged.at[chunk, peer],
                    y.at[:, columns(grp, chunk)],
                    s2.at[chunk, step],
                    r2.at[chunk, step],
                    (peer, blk),
                )
            else:
                copy = pltpu.make_async_copy(
                    staged.at[chunk, grp], y.at[:, columns(grp, chunk)], local2.at[chunk]
                )
            copy.start()
            second.append(copy)
    for copy in second:
        copy.wait()
    for row, copy in first:
        for copy in row:
            copy.wait_send()


def product(left, right):
    return jnp.dot(left.astype(BF16), right.astype(BF16), preferred_element_type=F32)


def local(
    info,
    g,
    left_old,
    right_old,
    left_stored,
    right_stored,
    left_out,
    right_out,
    left_root,
    right_root,
    u,
    stats,
    roots,
    moving,
    iterate,
    out_sem,
    done_sem,
):
    size = g.shape[0]
    count = jnp.max(info[...])
    weight = (1.0 - decay_rate) / size
    stores = []
    for side, (dims, old, ref) in enumerate(((1, left_old, left_out), (0, right_old, right_out))):
        gram = lax.dot_general(
            g[...], g[...], (((dims,), (dims,)), ((), ())), preferred_element_type=F32
        )
        stats[side] = decay_rate * old[...] + weight * gram
        stores.append(pltpu.make_async_copy(stats.at[side], ref, out_sem.at[side]))
        stores[-1].start()
    roots[0] = left_stored[...]
    roots[1] = right_stored[...]

    lead = (root_order + 1.0) / root_order
    square = lead * lead

    def unit(scale):
        rows = lax.broadcasted_iota(jnp.int32, (size, size), 0)
        cols = lax.broadcasted_iota(jnp.int32, (size, size), 1)
        return jnp.where(rows == cols, jnp.float32(scale), jnp.float32(0.0))

    def advance(m):
        part = product(m, m) / root_order**2 - (2.0 * lead / root_order) * m
        fourth = 2.0 * square * part + product(part, part)
        return square * square * m + product(fourth, m)

    @pl.when(count > 0)
    def refresh():
        scales = []
        for side in range(2):
            shifted = stats[side] + unit(damping)
            frobenius = jnp.sqrt(jnp.full((1, 1), jnp.sum(shifted * shifted), F32))
            scaling = (1.0 + root_order) / (2.0 * frobenius)
            scales.append(jnp.sqrt(jnp.sqrt(scaling)))
            moving[side] = scaling * shifted
            iterate[side] = unit(lead) - moving[side] / root_order

        @pl.when(count > 1)
        def again():
            for side in range(2):
                m = moving[side]
                after = advance(m)
                both = lead * after - product(m, after) / root_order
                moving[side] = after
                iterate[side] = lead * iterate[side] - both / root_order

        @pl.when(count > 2)
        def last():
            for side in range(2):
                y = iterate[side]
                iterate[side] = lead * y - product(y, advance(moving[side])) / root_order

        for side in range(2):
            roots[side] = (scales[side] * iterate[side]).astype(BF16)

    for side, ref in enumerate((left_root, right_root)):
        stores.append(pltpu.make_async_copy(roots.at[side], ref, done_sem.at[side]))
        stores[-1].start()
    half = jnp.dot(g[...], roots[1], preferred_element_type=F32).astype(BF16)
    precon = jnp.dot(roots[0], half, preferred_element_type=F32)
    wide = g[...].astype(F32)
    area = float(size * size)
    top = jnp.full((1, 1), jnp.sum(wide * wide), F32) / area
    bottom = jnp.full((1, 1), jnp.sum(precon * precon), F32) / area
    ratio = jnp.sqrt(top) / jnp.sqrt(bottom + 1e-06)
    u[...] = (precon * ratio).astype(BF16)
    for copy in stores:
        copy.wait()


HBM = pl.BlockSpec(memory_space=pltpu.HBM)
VMEM = pl.BlockSpec(memory_space=pltpu.VMEM)
DMA = pltpu.SemaphoreType.DMA


def per_device(
    gradient,
    stats_left,
    stats_right,
    root_left,
    root_right,
    slot_block,
    refresh_slots,
    newton_steps,
):
    groups = lax.axis_size("grp")
    owners = lax.axis_size("blk")
    rows = gradient.shape[0]
    size = stats_left.shape[1]
    share = groups // owners
    width = size // CHUNKS
    square = jax.ShapeDtypeStruct((size, size), F32)
    narrow = jax.ShapeDtypeStruct((size, size), BF16)
    picks = refresh_slots.shape[0]
    table = slot_block.T
    g, info, *held = pl.pallas_call(
        functools.partial(inbound, groups, owners, picks),
        name="inbound",
        out_shape=(
            jax.ShapeDtypeStruct((share, owners, rows, size), BF16),
            jax.ShapeDtypeStruct((8, 128), jnp.int32),
            square,
            square,
            narrow,
            narrow,
        ),
        in_specs=[HBM] * 8,
        out_specs=(VMEM,) * 6,
        scratch_shapes=[
            pltpu.SMEM(table.shape, jnp.int32),
            pltpu.SMEM((picks,), jnp.int32),
            pltpu.SMEM((picks,), jnp.int32),
            [pltpu.VMEM((groups, rows, width), BF16)] * CHUNKS,
            pltpu.VMEM((CHUNKS, owners, share, rows, width), BF16),
            DMA((CHUNKS,)),
            DMA((CHUNKS,)),
            DMA((CHUNKS, groups)),
            DMA((CHUNKS, groups)),
            DMA((CHUNKS, owners)),
            DMA((CHUNKS, owners)),
            DMA((3,)),
            DMA((4,)),
        ],
        compiler_params=pltpu.CompilerParams(
            collective_id=0, has_side_effects=True, vmem_limit_bytes=WIDE
        ),
    )(
        *(
            pltpu.with_memory_space_constraint(array, pltpu.HBM)
            for array in (
                table,
                refresh_slots,
                newton_steps,
                gradient,
                stats_left[0],
                stats_right[0],
                root_left[0],
                root_right[0],
            )
        )
    )
    left_new, right_new, left_root, right_root, u = pl.pallas_call(
        local,
        name="local",
        out_shape=(square, square, narrow, narrow, narrow),
        in_specs=[VMEM] * 6,
        out_specs=(HBM, HBM, HBM, HBM, VMEM),
        scratch_shapes=[
            pltpu.VMEM((2, size, size), F32),
            pltpu.VMEM((2, size, size), BF16),
            pltpu.VMEM((2, size, size), F32),
            pltpu.VMEM((2, size, size), F32),
            DMA((2,)),
            DMA((2,)),
        ],
        compiler_params=pltpu.CompilerParams(vmem_limit_bytes=GRANT),
    )(info, g.reshape(size, size), *held)
    y = pl.pallas_call(
        functools.partial(outbound, groups, owners),
        name="outbound",
        out_shape=jax.ShapeDtypeStruct(gradient.shape, BF16),
        in_specs=[HBM, VMEM],
        out_specs=VMEM,
        scratch_shapes=[
            pltpu.SMEM(table.shape, jnp.int32),
            [pltpu.VMEM((owners, share, rows, width), BF16)] * CHUNKS,
            pltpu.VMEM((CHUNKS, groups, rows, width), BF16),
            DMA((CHUNKS,)),
            DMA((CHUNKS,)),
            DMA((CHUNKS, owners)),
            DMA((CHUNKS, owners)),
            DMA((CHUNKS, groups)),
            DMA((CHUNKS, groups)),
            DMA,
        ],
        compiler_params=pltpu.CompilerParams(
            collective_id=1, has_side_effects=True, vmem_limit_bytes=SMALL
        ),
    )(pltpu.with_memory_space_constraint(table, pltpu.HBM), u.reshape(share, owners, rows, size))
    return (left_new[None], right_new[None], left_root[None], right_root[None], y)


def solution(mesh):
    placed = (
        P(("grp", "blk"), None),
        P(("grp", "blk"), None, None),
        P(("grp", "blk"), None, None),
        P(("grp", "blk"), None, None),
        P(("grp", "blk"), None, None),
        P(),
        P(),
        P(),
    )
    return jax.shard_map(
        per_device,
        mesh=mesh,
        in_specs=placed,
        out_specs=(
            P(("grp", "blk"), None, None),
            P(("grp", "blk"), None, None),
            P(("grp", "blk"), None, None),
            P(("grp", "blk"), None, None),
            P(("grp", "blk"), None),
        ),
        check_vma=False,
    )
```

```python
import functools

import jax
import jax.numpy as jnp
from jax import lax
from jax.experimental import pallas as pl
from jax.experimental.pallas import tpu as pltpu
from jax.sharding import PartitionSpec as P

damping = 0.0001
decay_rate = 0.9
root_order = 4.0
CHUNKS = 4
GRANT = 28 * 2**20
SMALL = 12 * 2**20
WIDE = 12 * 2**20
MESH = pl.DeviceIdType.MESH
F32 = jnp.float32
BF16 = jnp.bfloat16


def enter(groups, owners, grp, blk):
    barrier = pltpu.get_barrier_semaphore()
    for step in range(1, groups):
        peer = lax.rem(grp + step, groups)
        pl.semaphore_signal(barrier, inc=1, device_id=(peer, blk), device_id_type=MESH)
    for step in range(1, owners):
        peer = lax.rem(blk + step, owners)
        pl.semaphore_signal(barrier, inc=1, device_id=(grp, peer), device_id_type=MESH)
    pl.semaphore_wait(barrier, groups + owners - 2)


def remote(src, dst, send, recv, device):
    return pltpu.make_async_remote_copy(
        src_ref=src,
        dst_ref=dst,
        send_sem=send,
        recv_sem=recv,
        device_id=device,
        device_id_type=MESH,
    )


def inbound(groups, owners, picks, *refs):
    table, slots_in, steps_in, x = refs[:4]
    held_in, held = refs[4:8], refs[10:14]
    g, info = refs[8:10]
    order, slots, steps, landed, staged, local1, local2, s1, r1, s2, r2, small, large = refs[14:]
    grp, blk = lax.axis_index("grp"), lax.axis_index("blk")
    tables = []
    for place, (source, target) in enumerate(((table, order), (slots_in, slots), (steps_in, steps))):
        tables.append(pltpu.make_async_copy(source, target, small.at[place]))
        tables[-1].start()
    share = groups // owners
    block = landed[0].shape[-1] * CHUNKS
    width = landed[0].shape[-1]

    def columns(owner, chunk):
        return pl.ds(pl.multiple_of(owner * block + chunk * width, width), width)

    mine = []
    for chunk in range(CHUNKS):
        copy = pltpu.make_async_copy(
            x.at[:, columns(grp, chunk)], landed[chunk].at[grp], local1.at[chunk]
        )
        copy.start()
        mine.append(copy)
    enter(groups, owners, grp, blk)
    first = []
    for chunk in range(CHUNKS):
        row = []
        for step in range(1, groups):
            peer = lax.rem(grp + step, groups)
            copy = remote(
                x.at[:, columns(peer, chunk)],
                landed[chunk].at[grp],
                s1.at[chunk, step],
                r1.at[chunk, step],
                (peer, blk),
            )
            copy.start()
            row.append(copy)
        first.append(row)
    loads = []
    for place in range(4):
        loads.append(pltpu.make_async_copy(held_in[place], held[place], large.at[place]))
        loads[-1].start()
    for copy in tables:
        copy.wait()
    own = grp * owners + blk
    count = jnp.int32(0)
    for pick in range(picks):
        count = count + jnp.where(slots[pick] == own, steps[pick], 0)
    info[...] = jnp.full(info.shape, count, jnp.int32)
    second, arriving = [], []
    for chunk in range(CHUNKS):
        mine[chunk].wait()
        for copy in first[chunk]:
            copy.wait_recv()
        cut = pl.ds(chunk * width, width)
        for place in range(owners):
            peer = far_first(owners, blk, place) if place < owners - 1 else blk
            source = order[peer, grp] * share
            staged[chunk, peer] = landed[chunk][pl.ds(source, share)]
            if place < owners - 1:
                copy = remote(
                    staged.at[chunk, peer],
                    g.at[:, blk, :, cut],
                    s2.at[chunk, peer],
                    r2.at[chunk, blk],
                    (grp, peer),
                )
                arriving.append(
                    remote(
                        staged.at[chunk, peer],
                        g.at[:, peer, :, cut],
                        s2.at[chunk, peer],
                        r2.at[chunk, peer],
                        (grp, peer),
                    )
                )
            else:
                copy = pltpu.make_async_copy(
                    staged.at[chunk, blk], g.at[:, blk, :, cut], local2.at[chunk]
                )
            copy.start()
            second.append((copy, place < owners - 1))
    for copy, far in second:
        if far:
            copy.wait_send()
        else:
            copy.wait()
    for copy in arriving:
        copy.wait_recv()
    for copy in loads:
        copy.wait()
    for row in first:
        for copy in row:
            copy.wait_send()


def outbound(
    groups, owners, table, u, y, order, landed, staged, local1, local2, s1, r1, s2, r2, small
):
    grp, blk = lax.axis_index("grp"), lax.axis_index("blk")
    fetch = pltpu.make_async_copy(table, order, small)
    fetch.start()
    share = groups // owners
    width = landed[0].shape[-1]
    block = width * CHUNKS

    def columns(owner, chunk):
        return pl.ds(pl.multiple_of(owner * block + chunk * width, width), width)

    enter(groups, owners, grp, blk)
    first = []
    for chunk in range(CHUNKS):
        row = []
        cut = pl.ds(chunk * width, width)
        for place in range(owners - 1):
            peer = far_first(owners, blk, place)
            source = u.at[:, peer, :, cut]
            send = s1.at[chunk, peer]
            copy = remote(source, landed[chunk].at[blk], send, r1.at[chunk, blk], (grp, peer))
            copy.start()
            row.append(
                remote(source, landed[chunk].at[peer], send, r1.at[chunk, peer], (grp, peer))
            )
        copy = pltpu.make_async_copy(
            u.at[:, blk, :, cut], landed[chunk].at[blk], local1.at[chunk]
        )
        copy.start()
        first.append((row, copy))
    fetch.wait()
    places = []
    for position in range(owners):
        place = jnp.int32(0)
        for slot in range(owners):
            place = jnp.where(order[slot, grp] == position, slot, place)
        places.append(place)
    second = []
    for chunk in range(CHUNKS):
        row, copy = first[chunk]
        copy.wait()
        for copy in row:
            copy.wait_recv()
        for position in range(owners):
            for part in range(share):
                staged[chunk, position * share + part] = landed[chunk][places[position], part]
        for step in range(1, groups + 1):
            peer = lax.rem(grp + step, groups)
            if step < groups:
                copy = remote(
                    staged.at[chunk, peer],
                    y.at[:, columns(grp, chunk)],
                    s2.at[chunk, step],
                    r2.at[chunk, step],
                    (peer, blk),
                )
            else:
                copy = pltpu.make_async_copy(
                    staged.at[chunk, grp], y.at[:, columns(grp, chunk)], local2.at[chunk]
                )
            copy.start()
            second.append(copy)
    for copy in second:
        copy.wait()
    for row, copy in first:
        for copy in row:
            copy.wait_send()


def far_first(owners, blk, place):
    falling = owners - 1 - place
    falling = falling - jnp.where(falling <= blk, 1, 0)
    rising = place + jnp.where(place >= blk, 1, 0)
    return jnp.where(blk < owners // 2, falling, rising)


def commuting(left, right):
    left, right = left.astype(BF16), right.astype(BF16)
    half = left.shape[0] // 2
    top = jnp.dot(left[:half], right, preferred_element_type=F32)
    corner = jnp.dot(left[half:], right[:, half:], preferred_element_type=F32)
    bottom = jnp.concatenate([top[:, half:].T, corner], axis=1)
    return jnp.concatenate([top, bottom], axis=0)


def product(left, right):
    return jnp.dot(left.astype(BF16), right.astype(BF16), preferred_element_type=F32)


def local(
    info,
    g,
    left_old,
    right_old,
    left_stored,
    right_stored,
    left_out,
    right_out,
    left_root,
    right_root,
    u,
    stats,
    roots,
    moving,
    iterate,
    out_sem,
    done_sem,
):
    size = g.shape[0]
    count = jnp.max(info[...])
    weight = (1.0 - decay_rate) / size
    stores = []
    for side, (dims, old, ref) in enumerate(((1, left_old, left_out), (0, right_old, right_out))):
        gram = lax.dot_general(
            g[...], g[...], (((dims,), (dims,)), ((), ())), preferred_element_type=F32
        )
        stats[side] = decay_rate * old[...] + weight * gram
        stores.append(pltpu.make_async_copy(stats.at[side], ref, out_sem.at[side]))
        stores[-1].start()
    roots[0] = left_stored[...]
    roots[1] = right_stored[...]

    lead = (root_order + 1.0) / root_order
    square = lead * lead

    def unit(scale):
        rows = lax.broadcasted_iota(jnp.int32, (size, size), 0)
        cols = lax.broadcasted_iota(jnp.int32, (size, size), 1)
        return jnp.where(rows == cols, jnp.float32(scale), jnp.float32(0.0))

    def advance(m):
        part = commuting(m, m) / root_order**2 - (2.0 * lead / root_order) * m
        fourth = 2.0 * square * part + commuting(part, part)
        return square * square * m + commuting(fourth, m)

    @pl.when(count > 0)
    def refresh():
        scales = []
        for side in range(2):
            shifted = stats[side] + unit(damping)
            frobenius = jnp.sqrt(jnp.full((1, 1), jnp.sum(shifted * shifted), F32))
            scaling = (1.0 + root_order) / (2.0 * frobenius)
            scales.append(jnp.sqrt(jnp.sqrt(scaling)))
            moving[side] = scaling * shifted
            iterate[side] = unit(lead) - moving[side] / root_order

        @pl.when(count > 1)
        def again():
            for side in range(2):
                m = moving[side]
                after = advance(m)
                both = lead * after - commuting(m, after) / root_order
                moving[side] = after
                iterate[side] = lead * iterate[side] - both / root_order

        @pl.when(count > 2)
        def last():
            for side in range(2):
                y = iterate[side]
                iterate[side] = lead * y - commuting(y, advance(moving[side])) / root_order

        for side in range(2):
            roots[side] = (scales[side] * iterate[side]).astype(BF16)

    for side, ref in enumerate((left_root, right_root)):
        stores.append(pltpu.make_async_copy(roots.at[side], ref, done_sem.at[side]))
        stores[-1].start()
    half = jnp.dot(g[...], roots[1], preferred_element_type=F32).astype(BF16)
    precon = jnp.dot(roots[0], half, preferred_element_type=F32)
    wide = g[...].astype(F32)
    area = float(size * size)
    top = jnp.full((1, 1), jnp.sum(wide * wide), F32) / area
    bottom = jnp.full((1, 1), jnp.sum(precon * precon), F32) / area
    ratio = jnp.sqrt(top) / jnp.sqrt(bottom + 1e-06)
    u[...] = (precon * ratio).astype(BF16)
    for copy in stores:
        copy.wait()


HBM = pl.BlockSpec(memory_space=pltpu.HBM)
VMEM = pl.BlockSpec(memory_space=pltpu.VMEM)
DMA = pltpu.SemaphoreType.DMA


def per_device(
    gradient,
    stats_left,
    stats_right,
    root_left,
    root_right,
    slot_block,
    refresh_slots,
    newton_steps,
):
    groups = lax.axis_size("grp")
    owners = lax.axis_size("blk")
    rows = gradient.shape[0]
    size = stats_left.shape[1]
    share = groups // owners
    width = size // CHUNKS
    square = jax.ShapeDtypeStruct((size, size), F32)
    narrow = jax.ShapeDtypeStruct((size, size), BF16)
    picks = refresh_slots.shape[0]
    table = slot_block.T
    g, info, *held = pl.pallas_call(
        functools.partial(inbound, groups, owners, picks),
        name="inbound",
        out_shape=(
            jax.ShapeDtypeStruct((share, owners, rows, size), BF16),
            jax.ShapeDtypeStruct((8, 128), jnp.int32),
            square,
            square,
            narrow,
            narrow,
        ),
        in_specs=[HBM] * 8,
        out_specs=(VMEM,) * 6,
        scratch_shapes=[
            pltpu.SMEM(table.shape, jnp.int32),
            pltpu.SMEM((picks,), jnp.int32),
            pltpu.SMEM((picks,), jnp.int32),
            [pltpu.VMEM((groups, rows, width), BF16)] * CHUNKS,
            pltpu.VMEM((CHUNKS, owners, share, rows, width), BF16),
            DMA((CHUNKS,)),
            DMA((CHUNKS,)),
            DMA((CHUNKS, groups)),
            DMA((CHUNKS, groups)),
            DMA((CHUNKS, owners)),
            DMA((CHUNKS, owners)),
            DMA((3,)),
            DMA((4,)),
        ],
        compiler_params=pltpu.CompilerParams(
            collective_id=0, has_side_effects=True, vmem_limit_bytes=WIDE
        ),
    )(
        *(
            pltpu.with_memory_space_constraint(array, pltpu.HBM)
            for array in (
                table,
                refresh_slots,
                newton_steps,
                gradient,
                stats_left[0],
                stats_right[0],
                root_left[0],
                root_right[0],
            )
        )
    )
    left_new, right_new, left_root, right_root, u = pl.pallas_call(
        local,
        name="local",
        out_shape=(square, square, narrow, narrow, narrow),
        in_specs=[VMEM] * 6,
        out_specs=(HBM, HBM, HBM, HBM, VMEM),
        scratch_shapes=[
            pltpu.VMEM((2, size, size), F32),
            pltpu.VMEM((2, size, size), BF16),
            pltpu.VMEM((2, size, size), F32),
            pltpu.VMEM((2, size, size), F32),
            DMA((2,)),
            DMA((2,)),
        ],
        compiler_params=pltpu.CompilerParams(vmem_limit_bytes=GRANT),
    )(info, g.reshape(size, size), *held)
    y = pl.pallas_call(
        functools.partial(outbound, groups, owners),
        name="outbound",
        out_shape=jax.ShapeDtypeStruct(gradient.shape, BF16),
        in_specs=[HBM, VMEM],
        out_specs=VMEM,
        scratch_shapes=[
            pltpu.SMEM(table.shape, jnp.int32),
            [pltpu.VMEM((owners, share, rows, width), BF16)] * CHUNKS,
            pltpu.VMEM((CHUNKS, groups, rows, width), BF16),
            DMA((CHUNKS,)),
            DMA((CHUNKS,)),
            DMA((CHUNKS, owners)),
            DMA((CHUNKS, owners)),
            DMA((CHUNKS, groups)),
            DMA((CHUNKS, groups)),
            DMA,
        ],
        compiler_params=pltpu.CompilerParams(
            collective_id=1, has_side_effects=True, vmem_limit_bytes=SMALL
        ),
    )(pltpu.with_memory_space_constraint(table, pltpu.HBM), u.reshape(share, owners, rows, size))
    return (left_new[None], right_new[None], left_root[None], right_root[None], y)


def solution(mesh):
    placed = (
        P(("grp", "blk"), None),
        P(("grp", "blk"), None, None),
        P(("grp", "blk"), None, None),
        P(("grp", "blk"), None, None),
        P(("grp", "blk"), None, None),
        P(),
        P(),
        P(),
    )
    return jax.shard_map(
        per_device,
        mesh=mesh,
        in_specs=placed,
        out_specs=(
            P(("grp", "blk"), None, None),
            P(("grp", "blk"), None, None),
            P(("grp", "blk"), None, None),
            P(("grp", "blk"), None, None),
            P(("grp", "blk"), None),
        ),
        check_vma=False,
    )
```

```python
import functools

import jax
import jax.numpy as jnp
from jax import lax
from jax.experimental import pallas as pl
from jax.experimental.pallas import tpu as pltpu
from jax.sharding import PartitionSpec as P

damping = 0.0001
decay_rate = 0.9
root_order = 4.0
COLUMN_CUTS = 4
GRANT = 28 * 2**20
SMALL = 12 * 2**20
WIDE = 12 * 2**20
MESH = pl.DeviceIdType.MESH
F32 = jnp.float32
BF16 = jnp.bfloat16


def enter(groups, owners, grp, blk):
    barrier = pltpu.get_barrier_semaphore()
    for step in range(1, groups):
        peer = lax.rem(grp + step, groups)
        pl.semaphore_signal(barrier, inc=1, device_id=(peer, blk), device_id_type=MESH)
    for step in range(1, owners):
        peer = lax.rem(blk + step, owners)
        pl.semaphore_signal(barrier, inc=1, device_id=(grp, peer), device_id_type=MESH)
    pl.semaphore_wait(barrier, groups + owners - 2)


def remote(src, dst, send, recv, device):
    return pltpu.make_async_remote_copy(
        src_ref=src,
        dst_ref=dst,
        send_sem=send,
        recv_sem=recv,
        device_id=device,
        device_id_type=MESH,
    )


def inbound(groups, owners, picks, *refs):
    table, slots_in, steps_in, x = refs[:4]
    held_in, held = refs[4:8], refs[10:14]
    g, info = refs[8:10]
    order, slots, steps, landed, staged, local1, local2, s1, r1, s2, r2, small, large = refs[14:]
    grp, blk = lax.axis_index("grp"), lax.axis_index("blk")
    tables = []
    for place, (source, target) in enumerate(((table, order), (slots_in, slots), (steps_in, steps))):
        tables.append(pltpu.make_async_copy(source, target, small.at[place]))
        tables[-1].start()
    share = groups // owners
    width = landed[0].shape[-1]
    block = width * COLUMN_CUTS
    depth = landed[0].shape[-2]
    chunks = len(landed)

    def columns(owner, chunk):
        return pl.ds(pl.multiple_of(owner * block + chunk % COLUMN_CUTS * width, width), width)

    def lines(chunk):
        return pl.ds(chunk // COLUMN_CUTS * depth, depth)

    mine = []
    for chunk in range(chunks):
        copy = pltpu.make_async_copy(
            x.at[lines(chunk), columns(grp, chunk)], landed[chunk].at[grp], local1.at[chunk]
        )
        copy.start()
        mine.append(copy)
    enter(groups, owners, grp, blk)
    first = []
    for chunk in range(chunks):
        row = []
        for step in range(1, groups):
            peer = lax.rem(grp + step, groups)
            copy = remote(
                x.at[lines(chunk), columns(peer, chunk)],
                landed[chunk].at[grp],
                s1.at[chunk, step],
                r1.at[chunk, step],
                (peer, blk),
            )
            copy.start()
            row.append(copy)
        first.append(row)
    loads = []
    for place in range(4):
        loads.append(pltpu.make_async_copy(held_in[place], held[place], large.at[place]))
        loads[-1].start()
    for copy in tables:
        copy.wait()
    own = grp * owners + blk
    count = jnp.int32(0)
    for pick in range(picks):
        count = count + jnp.where(slots[pick] == own, steps[pick], 0)
    info[...] = jnp.full(info.shape, count, jnp.int32)
    second, arriving = [], []
    for chunk in range(chunks):
        mine[chunk].wait()
        for copy in first[chunk]:
            copy.wait_recv()
        cut = pl.ds(chunk % COLUMN_CUTS * width, width)
        for place in range(owners):
            peer = far_first(owners, blk, place) if place < owners - 1 else blk
            source = order[peer, grp] * share
            staged[chunk, peer] = landed[chunk][pl.ds(source, share)]
            if place < owners - 1:
                copy = remote(
                    staged.at[chunk, peer],
                    g.at[:, blk, lines(chunk), cut],
                    s2.at[chunk, peer],
                    r2.at[chunk, blk],
                    (grp, peer),
                )
                arriving.append(
                    remote(
                        staged.at[chunk, peer],
                        g.at[:, peer, lines(chunk), cut],
                        s2.at[chunk, peer],
                        r2.at[chunk, peer],
                        (grp, peer),
                    )
                )
            else:
                copy = pltpu.make_async_copy(
                    staged.at[chunk, blk], g.at[:, blk, lines(chunk), cut], local2.at[chunk]
                )
            copy.start()
            second.append((copy, place < owners - 1))
    for copy, far in second:
        if far:
            copy.wait_send()
        else:
            copy.wait()
    for copy in arriving:
        copy.wait_recv()
    for copy in loads:
        copy.wait()
    for row in first:
        for copy in row:
            copy.wait_send()


def outbound(
    groups, owners, table, u, y, order, landed, staged, local1, local2, s1, r1, s2, r2, small
):
    grp, blk = lax.axis_index("grp"), lax.axis_index("blk")
    fetch = pltpu.make_async_copy(table, order, small)
    fetch.start()
    share = groups // owners
    width = landed[0].shape[-1]
    block = width * COLUMN_CUTS
    depth = landed[0].shape[-2]
    chunks = len(landed)

    def columns(owner, chunk):
        return pl.ds(pl.multiple_of(owner * block + chunk % COLUMN_CUTS * width, width), width)

    def lines(chunk):
        return pl.ds(chunk // COLUMN_CUTS * depth, depth)

    enter(groups, owners, grp, blk)
    first = []
    for chunk in range(chunks):
        row = []
        cut = pl.ds(chunk % COLUMN_CUTS * width, width)
        for place in range(owners - 1):
            peer = far_first(owners, blk, place)
            source = u.at[:, peer, lines(chunk), cut]
            send = s1.at[chunk, peer]
            copy = remote(source, landed[chunk].at[blk], send, r1.at[chunk, blk], (grp, peer))
            copy.start()
            row.append(
                remote(source, landed[chunk].at[peer], send, r1.at[chunk, peer], (grp, peer))
            )
        copy = pltpu.make_async_copy(
            u.at[:, blk, lines(chunk), cut], landed[chunk].at[blk], local1.at[chunk]
        )
        copy.start()
        first.append((row, copy))
    fetch.wait()
    places = []
    for position in range(owners):
        place = jnp.int32(0)
        for slot in range(owners):
            place = jnp.where(order[slot, grp] == position, slot, place)
        places.append(place)
    second = []
    for chunk in range(chunks):
        row, copy = first[chunk]
        copy.wait()
        for copy in row:
            copy.wait_recv()
        for position in range(owners):
            for part in range(share):
                staged[chunk, position * share + part] = landed[chunk][places[position], part]
        for step in range(1, groups + 1):
            peer = lax.rem(grp + step, groups)
            if step < groups:
                copy = remote(
                    staged.at[chunk, peer],
                    y.at[lines(chunk), columns(grp, chunk)],
                    s2.at[chunk, step],
                    r2.at[chunk, step],
                    (peer, blk),
                )
            else:
                copy = pltpu.make_async_copy(
                    staged.at[chunk, grp], y.at[lines(chunk), columns(grp, chunk)], local2.at[chunk]
                )
            copy.start()
            second.append(copy)
    for copy in second:
        copy.wait()
    for row, copy in first:
        for copy in row:
            copy.wait_send()


def far_first(owners, blk, place):
    falling = owners - 1 - place
    falling = falling - jnp.where(falling <= blk, 1, 0)
    rising = place + jnp.where(place >= blk, 1, 0)
    return jnp.where(blk < owners // 2, falling, rising)


def commuting(left, right):
    left, right = left.astype(BF16), right.astype(BF16)
    half = left.shape[0] // 2
    top = jnp.dot(left[:half], right, preferred_element_type=F32)
    corner = jnp.dot(left[half:], right[:, half:], preferred_element_type=F32)
    bottom = jnp.concatenate([top[:, half:].T, corner], axis=1)
    return jnp.concatenate([top, bottom], axis=0)


def product(left, right):
    return jnp.dot(left.astype(BF16), right.astype(BF16), preferred_element_type=F32)


def local(
    info,
    g,
    left_old,
    right_old,
    left_stored,
    right_stored,
    left_out,
    right_out,
    left_root,
    right_root,
    u,
    stats,
    roots,
    moving,
    iterate,
    out_sem,
    done_sem,
):
    size = g.shape[0]
    count = jnp.max(info[...])
    weight = (1.0 - decay_rate) / size
    stores = []
    for side, (dims, old, ref) in enumerate(((1, left_old, left_out), (0, right_old, right_out))):
        gram = lax.dot_general(
            g[...], g[...], (((dims,), (dims,)), ((), ())), preferred_element_type=F32
        )
        stats[side] = decay_rate * old[...] + weight * gram
        stores.append(pltpu.make_async_copy(stats.at[side], ref, out_sem.at[side]))
        stores[-1].start()
    roots[0] = left_stored[...]
    roots[1] = right_stored[...]

    lead = (root_order + 1.0) / root_order
    square = lead * lead

    def unit(scale):
        rows = lax.broadcasted_iota(jnp.int32, (size, size), 0)
        cols = lax.broadcasted_iota(jnp.int32, (size, size), 1)
        return jnp.where(rows == cols, jnp.float32(scale), jnp.float32(0.0))

    def advance(m):
        part = commuting(m, m) / root_order**2 - (2.0 * lead / root_order) * m
        fourth = 2.0 * square * part + commuting(part, part)
        return square * square * m + commuting(fourth, m)

    @pl.when(count > 0)
    def refresh():
        scales = []
        for side in range(2):
            shifted = stats[side] + unit(damping)
            frobenius = jnp.sqrt(jnp.full((1, 1), jnp.sum(shifted * shifted), F32))
            scaling = (1.0 + root_order) / (2.0 * frobenius)
            scales.append(jnp.sqrt(jnp.sqrt(scaling)))
            moving[side] = scaling * shifted
            iterate[side] = unit(lead) - moving[side] / root_order

        @pl.when(count > 1)
        def again():
            for side in range(2):
                m = moving[side]
                after = advance(m)
                both = lead * after - commuting(m, after) / root_order
                moving[side] = after
                iterate[side] = lead * iterate[side] - both / root_order

        @pl.when(count > 2)
        def last():
            for side in range(2):
                y = iterate[side]
                iterate[side] = lead * y - commuting(y, advance(moving[side])) / root_order

        for side in range(2):
            roots[side] = (scales[side] * iterate[side]).astype(BF16)

    for side, ref in enumerate((left_root, right_root)):
        stores.append(pltpu.make_async_copy(roots.at[side], ref, done_sem.at[side]))
        stores[-1].start()
    half = jnp.dot(g[...], roots[1], preferred_element_type=F32).astype(BF16)
    precon = jnp.dot(roots[0], half, preferred_element_type=F32)
    wide = g[...].astype(F32)
    area = float(size * size)
    top = jnp.full((1, 1), jnp.sum(wide * wide), F32) / area
    bottom = jnp.full((1, 1), jnp.sum(precon * precon), F32) / area
    ratio = jnp.sqrt(top) / jnp.sqrt(bottom + 1e-06)
    u[...] = (precon * ratio).astype(BF16)
    for copy in stores:
        copy.wait()


HBM = pl.BlockSpec(memory_space=pltpu.HBM)
VMEM = pl.BlockSpec(memory_space=pltpu.VMEM)
DMA = pltpu.SemaphoreType.DMA


def per_device(
    gradient,
    stats_left,
    stats_right,
    root_left,
    root_right,
    slot_block,
    refresh_slots,
    newton_steps,
):
    groups = lax.axis_size("grp")
    owners = lax.axis_size("blk")
    rows = gradient.shape[0]
    size = stats_left.shape[1]
    share = groups // owners
    width = size // COLUMN_CUTS
    cuts = 2 if rows % 32 == 0 else 1
    chunks, depth = COLUMN_CUTS * cuts, rows // cuts
    square = jax.ShapeDtypeStruct((size, size), F32)
    narrow = jax.ShapeDtypeStruct((size, size), BF16)
    picks = refresh_slots.shape[0]
    table = slot_block.T
    g, info, *held = pl.pallas_call(
        functools.partial(inbound, groups, owners, picks),
        name="inbound",
        out_shape=(
            jax.ShapeDtypeStruct((share, owners, rows, size), BF16),
            jax.ShapeDtypeStruct((8, 128), jnp.int32),
            square,
            square,
            narrow,
            narrow,
        ),
        in_specs=[HBM] * 8,
        out_specs=(VMEM,) * 6,
        scratch_shapes=[
            pltpu.SMEM(table.shape, jnp.int32),
            pltpu.SMEM((picks,), jnp.int32),
            pltpu.SMEM((picks,), jnp.int32),
            [pltpu.VMEM((groups, depth, width), BF16)] * chunks,
            pltpu.VMEM((chunks, owners, share, depth, width), BF16),
            DMA((chunks,)),
            DMA((chunks,)),
            DMA((chunks, groups)),
            DMA((chunks, groups)),
            DMA((chunks, owners)),
            DMA((chunks, owners)),
            DMA((3,)),
            DMA((4,)),
        ],
        compiler_params=pltpu.CompilerParams(
            collective_id=0, has_side_effects=True, vmem_limit_bytes=WIDE
        ),
    )(
        *(
            pltpu.with_memory_space_constraint(array, pltpu.HBM)
            for array in (
                table,
                refresh_slots,
                newton_steps,
                gradient,
                stats_left[0],
                stats_right[0],
                root_left[0],
                root_right[0],
            )
        )
    )
    left_new, right_new, left_root, right_root, u = pl.pallas_call(
        local,
        name="local",
        out_shape=(square, square, narrow, narrow, narrow),
        in_specs=[VMEM] * 6,
        out_specs=(HBM, HBM, HBM, HBM, VMEM),
        scratch_shapes=[
            pltpu.VMEM((2, size, size), F32),
            pltpu.VMEM((2, size, size), BF16),
            pltpu.VMEM((2, size, size), F32),
            pltpu.VMEM((2, size, size), F32),
            DMA((2,)),
            DMA((2,)),
        ],
        compiler_params=pltpu.CompilerParams(vmem_limit_bytes=GRANT),
    )(info, g.reshape(size, size), *held)
    y = pl.pallas_call(
        functools.partial(outbound, groups, owners),
        name="outbound",
        out_shape=jax.ShapeDtypeStruct(gradient.shape, BF16),
        in_specs=[HBM, VMEM],
        out_specs=VMEM,
        scratch_shapes=[
            pltpu.SMEM(table.shape, jnp.int32),
            [pltpu.VMEM((owners, share, depth, width), BF16)] * chunks,
            pltpu.VMEM((chunks, groups, depth, width), BF16),
            DMA((chunks,)),
            DMA((chunks,)),
            DMA((chunks, owners)),
            DMA((chunks, owners)),
            DMA((chunks, groups)),
            DMA((chunks, groups)),
            DMA,
        ],
        compiler_params=pltpu.CompilerParams(
            collective_id=1, has_side_effects=True, vmem_limit_bytes=SMALL
        ),
    )(pltpu.with_memory_space_constraint(table, pltpu.HBM), u.reshape(share, owners, rows, size))
    return (left_new[None], right_new[None], left_root[None], right_root[None], y)


def solution(mesh):
    placed = (
        P(("grp", "blk"), None),
        P(("grp", "blk"), None, None),
        P(("grp", "blk"), None, None),
        P(("grp", "blk"), None, None),
        P(("grp", "blk"), None, None),
        P(),
        P(),
        P(),
    )
    return jax.shard_map(
        per_device,
        mesh=mesh,
        in_specs=placed,
        out_specs=(
            P(("grp", "blk"), None, None),
            P(("grp", "blk"), None, None),
            P(("grp", "blk"), None, None),
            P(("grp", "blk"), None, None),
            P(("grp", "blk"), None),
        ),
        check_vma=False,
    )
```
